32 devices in a mesh: dp: 8 (over z, x), tensor: 4 (over y, core).
Axes of the slice: x: 2, y: 2, z: 4, core: 2. Of those that a mesh axis runs over, the one named last changes fastest.
Arguments:
- inputs: bfloat16 [2048, 8192], P('dp', 'tensor'), may hold values from -6 to 6
- out_grads: bfloat16 [2048, 8192], P('dp', 'tensor'), may hold values from -6 to 6
- gate_pre: bfloat16 [2048, 28672], P('dp', 'tensor'), may hold values from -6 to 6
- up_pre: bfloat16 [2048, 28672], P('dp', 'tensor'), may hold values from -6 to 6
- hidden_grad: bfloat16 [2048, 28672], P('dp', 'tensor'), may hold values from -6 to 6
- proj_model: bfloat16 [8192, 128], P(('tensor', 'dp')), may hold values from -0.0625 to 0.0625
- proj_hidden: bfloat16 [28672, 192], P(('tensor', 'dp')), may hold values from -0.03125 to 0.03125
- lengths: int32 [8, 4], P('dp'), may hold values from 1 to 192, 256 in all within a row
- owners: int32 [8, 4], P('dp'), may hold values from 0 to 3, each once within a row
Outputs:
- features: float32 [32, 12288], P(('dp', 'tensor'))
The draws below stay inside these ranges and needn't reach their ends.
Inputs may be any that keep to these rules, and one draw needn't show every extreme that they name: `lengths`: each row sums to 256, and each row has an example of exactly 192 tokens. `owners`: each row names every slot once.
All inputs are finite; a program needn't handle non-finite values.
Results may differ from the reference program's by a relative error of at most 0.0029.
Values may be sent and summed in bfloat16 or wider, within the bound.
A program may use at most 64 MiB of HBM per device.

```python
import math
import jax
import jax.numpy as jnp
import numpy as np
from jax import lax

D = 8192
FF = 28672
RANK = 64
TOK_DEV = 256
MOST = 192
TOKENS = 2048
EXAMPLES = 32
FEAT = 12288
N_DP = 8
N_TENSOR = 4


def level_of(key, extent, pieces, low, largest):
    def one(axis_at, shards_of):
        steps = jax.random.uniform(jax.random.fold_in(jax.random.fold_in(key, 6), axis_at), (shards_of,), jnp.float32, low / len(pieces), largest / len(pieces))
        return jnp.repeat(jnp.exp(steps), extent[axis_at] // shards_of).reshape((-1,) + (1,) * (len(extent) - axis_at - 1))

    level = one(*pieces[0])
    for cut in pieces[1:]:
        level = level * one(*cut)
    return level


def length_profile(amount, total, limit, skew):
    loads = [(1 << 20) // math.isqrt(standing ** skew) + 1 for standing in range(2, amount + 1)]
    spare, given = total - limit - (amount - 1), [1] * (amount - 1)
    while spare > 0:
        movable = [i for i in range(amount - 1) if given[i] < limit]
        whole, budget = sum([loads[i] for i in movable]), spare
        for i in movable:
            more = min(limit - given[i], max(1, budget * loads[i] // whole), spare)
            given[i] = given[i] + more
            spare = spare - more
    return np.array([limit] + given)


def ragged(key, count, total, most, skew):
    if count == 2:
        one = jax.random.randint(key, (), max(1, total - most), min(most, total - 1) + 1)
        return jnp.stack([one, total - one])
    sizes = jnp.asarray(length_profile(count, total, most, skew), jnp.int32)
    twos = (count - 1) // 2
    giver, sink = sizes[1:1 + 2 * twos:2], sizes[2:2 + 2 * twos:2]
    slack = jnp.minimum(giver - 1, most - sink)
    passed = jax.random.randint(jax.random.fold_in(key, 1), (twos,), 0, 1 << 20) % (slack + 1)
    sizes = sizes.at[1:1 + 2 * twos:2].set(giver - passed).at[2:2 + 2 * twos:2].set(sink + passed)
    return sizes[jax.random.permutation(jax.random.fold_in(key, 2), count)]


def scatter_about(rng, dims, deviation, reach, shards=(), kind=jnp.bfloat16):
    drawn = deviation * jax.random.normal(rng, dims, jnp.float32)
    if shards:
        drawn = drawn * level_of(rng, dims, shards, -0.22, 0.18)
    return jnp.clip(drawn, -reach, reach).astype(kind)


def setup_inputs(seed: int = 0) -> dict:
    arg_keys = jax.random.split(jax.random.key(seed), 10)
    inputs = scatter_about(arg_keys[0], (TOKENS, D), 1.0, 6.0, ((0, 8), (1, 4)))
    out_grads = scatter_about(arg_keys[1], (TOKENS, D), 1.0, 6.0, ((0, 8), (1, 4)))
    gate_pre = scatter_about(arg_keys[2], (TOKENS, FF), 1.0, 6.0, ((0, 8), (1, 4)))
    up_pre = scatter_about(arg_keys[3], (TOKENS, FF), 1.0, 6.0, ((0, 8), (1, 4)))
    hidden_grad = scatter_about(arg_keys[4], (TOKENS, FF), 1.0, 6.0, ((0, 8), (1, 4)))
    proj_model = scatter_about(arg_keys[5], (D, 2 * RANK), D ** -0.5, 0.0625, ((0, 32),))
    proj_hidden = scatter_about(arg_keys[6], (FF, 3 * RANK), FF ** -0.5, 0.03125, ((0, 32),))
    lengths = jax.vmap(lambda own: ragged(own, N_TENSOR, TOK_DEV, MOST, 2))(jax.random.split(arg_keys[7], N_DP)).reshape((N_DP, N_TENSOR)).astype(jnp.int32)
    owners = jax.vmap(lambda own: jax.random.permutation(own, N_TENSOR))(jax.random.split(arg_keys[8], N_DP)).reshape((N_DP, N_TENSOR)).astype(jnp.int32)
    return {"inputs": inputs, "out_grads": out_grads, "gate_pre": gate_pre, "up_pre": up_pre, "hidden_grad": hidden_grad, "proj_model": proj_model, "proj_hidden": proj_hidden, "lengths": lengths, "owners": owners}


def one_group(group, proj_model, proj_hidden):
    inputs, out_grads, gate_pre, up_pre, hidden_grad, lens, owner_row = group
    gate_value = gate_pre.astype(jnp.float32)
    up_value = up_pre.astype(jnp.float32)
    grad_value = hidden_grad.astype(jnp.float32)
    sigmoid_gate = jax.nn.sigmoid(gate_value)
    hidden = (gate_value * sigmoid_gate * up_value).astype(jnp.bfloat16)
    up_grad = (grad_value * gate_value * sigmoid_gate).astype(jnp.bfloat16)
    gate_grad = (grad_value * up_value * sigmoid_gate * (1.0 + gate_value * (1.0 - sigmoid_gate))).astype(jnp.bfloat16)
    gate_out = jnp.dot(gate_grad, proj_hidden[:, :RANK], preferred_element_type=jnp.float32)
    up_out = jnp.dot(up_grad, proj_hidden[:, RANK:2 * RANK], preferred_element_type=jnp.float32)
    hidden_in = jnp.dot(hidden, proj_hidden[:, 2 * RANK:], preferred_element_type=jnp.float32)
    model_in = jnp.dot(inputs, proj_model[:, :RANK], preferred_element_type=jnp.float32)
    model_out = jnp.dot(out_grads, proj_model[:, RANK:], preferred_element_type=jnp.float32)
    starts = (jnp.cumsum(lens) - lens).astype(jnp.int32)
    places = jnp.arange(TOK_DEV, dtype=jnp.int32)
    masks = ((places[None, :] >= starts[:, None]) & (places[None, :] < (starts + lens)[:, None])).astype(jnp.float32)
    pairs = ((gate_out, model_in), (up_out, model_in), (model_out, hidden_in))
    blocks = [jnp.einsum("et,ta,tb->eab", masks, left_side, right_side, precision=lax.Precision.HIGHEST) for left_side, right_side in pairs]
    feats = jnp.stack(blocks, axis=1).reshape(N_TENSOR, FEAT)
    return jnp.zeros_like(feats).at[owner_row].set(feats)


def reference(inputs, out_grads, gate_pre, up_pre, hidden_grad, proj_model, proj_hidden, lengths, owners):
    grouped = (
        inputs.reshape(N_DP, TOK_DEV, D),
        out_grads.reshape(N_DP, TOK_DEV, D),
        gate_pre.reshape(N_DP, TOK_DEV, FF),
        up_pre.reshape(N_DP, TOK_DEV, FF),
        hidden_grad.reshape(N_DP, TOK_DEV, FF),
        lengths,
        owners,
    )
    result = lax.map(lambda group: one_group(group, proj_model, proj_hidden), grouped)
    return result.reshape(EXAMPLES, FEAT)
```

```python
import functools
import math

import jax
import jax.numpy as jnp
from jax import lax
from jax.experimental import pallas as pl
from jax.experimental.pallas import tpu as pltpu
from jax.sharding import PartitionSpec as P

MESH = pl.DeviceIdType.MESH
NT = (((1,), (1,)), ((), ()))
TN = (((0,), (0,)), ((), ()))
F32 = jnp.float32
BF16 = jnp.bfloat16
ROWS = 32


def kernel(
    nz, nx, ny,
    inp_h, og_h, gp_h, up_h, hg_h, pm_h, wt_h, lens, owns,
    out,
    raw, act, inp_v, og_v, pmb, whb, wgb, acc, part, rx1, chip, sx2, rx2, full, fs,
    raw_sem, io_sem, own_sem, recv, s_up, s_dn, s_x, r_sem, t_sem, r2_sem, t2_sem,
):
    ndp = nz * nx
    me = lax.axis_index("dp")
    t = lax.axis_index("tensor")
    z, x = me // nx, me % nx
    y, c = t // 2, t % 2
    mate = y * 2 + 1 - c
    units = wt_h.shape[1]
    feats = pm_h.shape[0]
    toks = inp_h.shape[0]
    half = toks // 2
    sources = (gp_h, up_h, hg_h)

    def raw_copy(block, slot, q):
        cols = pl.ds(pl.multiple_of(block * units, 128), units)
        return pltpu.make_async_copy(sources[q].at[:, cols], raw.at[slot, q], raw_sem.at[slot, q])

    for q in range(3):
        raw_copy(0, 0, q).start()
    io = (pltpu.make_async_copy(inp_h, inp_v, io_sem.at[0]),
          pltpu.make_async_copy(og_h, og_v, io_sem.at[1]))
    bufs = (pmb, whb, wgb)
    own = (pm_h, wt_h.at[pl.ds(128, 64), :], wt_h.at[pl.ds(0, 128), :])

    barrier = pltpu.get_barrier_semaphore()

    def greet(d, s):
        pl.semaphore_signal(barrier, inc=1, device_id=(d, s), device_id_type=MESH)

    for j in range(1, nx):
        greet(z * nx + (x + j) % nx, t)
    for j in range(1, ny):
        greet(me, ((y + j) % ny) * 2 + c)
    greet(me, mate)

    @pl.when(z < nz - 1)
    def _():
        greet(me + nx, t)

    @pl.when(z > 0)
    def _():
        greet(me - nx, t)

    pl.semaphore_wait(
        barrier, nx + ny - 1 + (z < nz - 1).astype(jnp.int32) + (z > 0).astype(jnp.int32)
    )

    def remote(p, src, slot, sem, d):
        return pltpu.make_async_remote_copy(
            src_ref=src, dst_ref=bufs[p].at[slot], send_sem=sem, recv_sem=recv.at[slot, p],
            device_id=(d, t), device_id_type=MESH,
        )

    def across(p, src, slot, j):
        return remote(p, src, slot, s_x.at[slot, p, j - 1], z * nx + (x + j) % nx)

    def upward(p, src, slot):
        return remote(p, src, slot, s_up.at[slot, p], me + nx)

    def downward(p, src, slot):
        return remote(p, src, slot, s_dn.at[slot, p], me - nx)

    for p in range(3):
        @pl.when(z < nz - 1)
        def _():
            upward(p, own[p], me).start()

        @pl.when(z > 0)
        def _():
            downward(p, own[p], me).start()

        for j in range(1, nx):
            across(p, own[p], me, j).start()
    keep = [pltpu.make_async_copy(own[p], bufs[p].at[me], own_sem.at[p]) for p in range(3)]
    for p in range(3):
        keep[p].start()
    for copy in io:
        copy.start()
    acc[...] = jnp.zeros_like(acc)

    def elementwise(block, carry):
        slot = block % 2

        @pl.when(block + 1 < ndp)
        def _():
            for q in range(3):
                raw_copy(block + 1, 1 - slot, q).start()

        for q in range(3):
            raw_copy(block, slot, q).wait()

        def some(i, carry):
            rows = pl.ds(pl.multiple_of(i * ROWS, ROWS), ROWS)
            gate = raw[slot, 0, rows, :].astype(F32)
            up = raw[slot, 1, rows, :].astype(F32)
            grad = raw[slot, 2, rows, :].astype(F32)
            sig = 0.5 * jnp.tanh(0.5 * gate) + 0.5
            silu = gate * sig
            act[0, block, rows, :] = (grad * up * (sig + silu * (1.0 - sig))).astype(BF16)
            act[1, block, rows, :] = (grad * silu).astype(BF16)
            act[2, block, rows, :] = (silu * up).astype(BF16)
            return carry

        lax.fori_loop(0, toks // ROWS, some, 0)
        return carry

    lax.fori_loop(0, ndp, elementwise, 0)
    for copy in io:
        copy.wait()
    for p in range(3):
        keep[p].wait()

    def dots(slot):
        cols = pl.ds(pl.multiple_of(slot * feats, 128), feats)
        weights = pmb[slot]
        acc[0] += lax.dot_general(act[0, slot], wgb[slot], NT, preferred_element_type=F32)
        acc[1] += lax.dot_general(act[1, slot], wgb[slot], NT, preferred_element_type=F32)
        acc[2] += jnp.dot(inp_v[:, cols], weights, preferred_element_type=F32)
        acc[3] += jnp.dot(og_v[:, cols], weights, preferred_element_type=F32)
        acc[4, :, pl.ds(0, 64)] += lax.dot_general(
            act[2, slot], whb[slot], NT, preferred_element_type=F32
        )

    near = jnp.minimum(z, nz - 1 - z)

    def plane(i):
        k = (i + 1) // 2
        paired = jnp.where(i % 2 == 1, z + k, z - k)
        far = jnp.where(z < nz - 1 - z, z + i - near, z - i + near)
        return jnp.where(i <= 2 * near, paired, far)

    def step(i, carry):
        @pl.when(i < nz)
        def _():
            src_z = plane(i)
            slot = src_z * nx + x

            @pl.when(i > 0)
            def _():
                for p in range(3):
                    block = bufs[p].at[slot]
                    across(p, block, slot, 1).wait_recv()

                    @pl.when((src_z < z) & (z < nz - 1))
                    def _():
                        upward(p, block, slot).start()

                    @pl.when((src_z > z) & (z > 0))
                    def _():
                        downward(p, block, slot).start()

                    for j in range(1, nx):
                        across(p, block, slot, j).start()

            dots(slot)

        @pl.when(i > 0)
        def _():
            for j in range(1, nx):
                slot = plane(i - 1) * nx + (x + j) % nx
                for p in range(3):
                    across(p, bufs[p].at[slot], slot, 1).wait_recv()
                dots(slot)

        return carry

    lax.fori_loop(0, nz + 1, step, 0)

    low = lax.broadcasted_iota(jnp.int32, (toks, 128), 1) < 64
    part[0] = jnp.where(low, acc[0], acc[1])
    part[1] = jnp.where(low, acc[2], acc[3])
    part[2] = acc[4]
    mine = pl.ds(pl.multiple_of(c * half, half), half)
    other = pl.ds(pl.multiple_of((1 - c) * half, half), half)
    first = pltpu.make_async_remote_copy(
        src_ref=part.at[:, other, :], dst_ref=rx1, send_sem=t_sem.at[0], recv_sem=r_sem.at[0],
        device_id=(me, mate), device_id_type=MESH,
    )
    first.start()
    first.wait_recv()
    both = part[:, mine, :] + rx1[...]
    chip[...] = both
    sx2[...] = both.astype(BF16)
    swaps = [
        pltpu.make_async_remote_copy(
            src_ref=sx2, dst_ref=rx2.at[j - 1], send_sem=t2_sem.at[j - 1],
            recv_sem=r2_sem.at[j - 1],
            device_id=(me, ((y + j) % ny) * 2 + c), device_id_type=MESH,
        )
        for j in range(1, ny)
    ]
    for copy in swaps:
        copy.start()
    for copy in swaps:
        copy.wait_recv()
    whole = chip[...]
    for j in range(1, ny):
        whole = whole + rx2[j - 1].astype(F32)
    full[c] = whole
    last = pltpu.make_async_remote_copy(
        src_ref=full.at[c], dst_ref=full.at[c], send_sem=t_sem.at[1], recv_sem=r_sem.at[1],
        device_id=(me, mate), device_id_type=MESH,
    )
    last.start()

    start, length, seen = jnp.int32(0), jnp.int32(0), jnp.int32(0)
    for e in range(2 * ny):
        hit = owns[0, e] == t
        start = jnp.where(hit, seen, start)
        length = jnp.where(hit, lens[0, e], length)
        seen = seen + lens[0, e]
    last.wait_recv()

    places = lax.broadcasted_iota(jnp.int32, (half, 128), 0)
    pair_one = jnp.zeros((128, 128), F32)
    pair_two = jnp.zeros((128, 128), F32)
    for h in range(2):
        token = places + h * half
        inside = (token >= start) & (token < start + length)
        model = full[h, 1]
        pair_one += lax.dot_general(
            jnp.where(inside, full[h, 0], 0.0), model, TN,
            precision=lax.Precision.HIGHEST, preferred_element_type=F32,
        )
        pair_two += lax.dot_general(
            jnp.where(inside, model, 0.0), full[h, 2], TN,
            precision=lax.Precision.HIGHEST, preferred_element_type=F32,
        )
    fs[pl.ds(0, 128), :] = pair_one
    fs[pl.ds(128, 64), :] = pair_two[64:, :]
    even = fs[pl.ds(0, 96, stride=2), :]
    odd = fs[pl.ds(1, 96, stride=2), :]
    out[...] = jnp.concatenate([even[:, :64], odd[:, :64]], axis=1)

    first.wait_send()
    last.wait_send()
    for copy in swaps:
        copy.wait_send()

    def drain(src_z, carry):
        slot = src_z * nx + x
        for p in range(3):
            block = bufs[p].at[slot]

            @pl.when((src_z <= z) & (z < nz - 1))
            def _():
                upward(p, block, slot).wait_send()

            @pl.when((src_z >= z) & (z > 0))
            def _():
                downward(p, block, slot).wait_send()

            for j in range(1, nx):
                across(p, block, slot, j).wait_send()
        return carry

    lax.fori_loop(0, nz, drain, 0)


def fused(
    nz, nx, ny,
    inputs, out_grads, gate_pre, up_pre, hidden_grad, proj_model, proj_hidden, lengths, owners,
):
    ndp = nz * nx
    toks, wide = inputs.shape
    units, feats = proj_hidden.shape[0], proj_model.shape[0]
    half = toks // 2
    hbm = pl.BlockSpec(memory_space=pltpu.HBM)
    smem = pl.BlockSpec(memory_space=pltpu.SMEM)
    dma = pltpu.SemaphoreType.DMA
    out = pl.pallas_call(
        functools.partial(kernel, nz, nx, ny),
        out_shape=jax.ShapeDtypeStruct((96, 128), F32),
        in_specs=[hbm] * 7 + [smem] * 2,
        out_specs=pl.BlockSpec(memory_space=pltpu.VMEM),
        scratch_shapes=[
            pltpu.VMEM((2, 3, toks, units), BF16),
            pltpu.VMEM((3, ndp, toks, units), BF16),
            pltpu.VMEM((toks, wide), BF16),
            pltpu.VMEM((toks, wide), BF16),
            pltpu.VMEM((ndp, feats, 128), BF16),
            pltpu.VMEM((ndp, 64, units), BF16),
            pltpu.VMEM((ndp, 128, units), BF16),
            pltpu.VMEM((5, toks, 128), F32),
            pltpu.VMEM((3, toks, 128), F32),
            pltpu.VMEM((3, half, 128), F32),
            pltpu.VMEM((3, half, 128), F32),
            pltpu.VMEM((3, half, 128), BF16),
            pltpu.VMEM((ny - 1, 3, half, 128), BF16),
            pltpu.VMEM((2, 3, half, 128), F32),
            pltpu.VMEM((192, 128), F32),
            dma((2, 3)),
            dma((2,)),
            dma((3,)),
            dma((ndp, 3)),
            dma((ndp, 3)),
            dma((ndp, 3)),
            dma((ndp, 3, nx - 1)),
            dma((2,)),
            dma((2,)),
            dma((ny - 1,)),
            dma((ny - 1,)),
        ],
        compiler_params=pltpu.CompilerParams(
            collective_id=0, has_side_effects=True, vmem_limit_bytes=48 << 20
        ),
    )(inputs, out_grads, gate_pre, up_pre, hidden_grad, proj_model, proj_hidden.T, lengths, owners)
    return out.reshape(1, 3 * 64 * 64)


def per_device(
    inputs, out_grads, gate_pre, up_pre, hidden_grad, proj_model, proj_hidden, lengths, owners
):
    rank_width = proj_model.shape[1] // 2
    tok_rows = inputs.shape[0]
    gate_value = gate_pre.astype(jnp.float32)
    up_value = up_pre.astype(jnp.float32)
    grad_value = hidden_grad.astype(jnp.float32)
    sigmoid_gate = jax.nn.sigmoid(gate_value)
    hidden = (gate_value * sigmoid_gate * up_value).astype(jnp.bfloat16)
    up_grad = (grad_value * gate_value * sigmoid_gate).astype(jnp.bfloat16)
    gate_grad = (
        grad_value * up_value * sigmoid_gate * (1.0 + gate_value * (1.0 - sigmoid_gate))
    ).astype(jnp.bfloat16)
    sources = (gate_grad, up_grad, hidden)
    block_rows = lax.all_gather(proj_hidden, "dp", axis=0, tiled=True)
    parts = []
    for column, source in enumerate(sources):
        parts.append(
            jnp.dot(
                source,
                block_rows[:, column * rank_width : (column + 1) * rank_width],
                preferred_element_type=jnp.float32,
            )
        )
    hidden_part = jnp.concatenate(parts, axis=1)
    block_rows = lax.all_gather(proj_model, "dp", axis=0, tiled=True)
    first_part = jnp.dot(inputs, block_rows[:, :rank_width], preferred_element_type=jnp.float32)
    second_part = jnp.dot(out_grads, block_rows[:, rank_width:], preferred_element_type=jnp.float32)
    model_part = jnp.concatenate([first_part, second_part], axis=1)
    partial_value = jnp.concatenate([hidden_part, model_part], axis=1)
    lens = lengths[0]
    owner_row = owners[0]
    starts = jnp.cumsum(lens) - lens
    myself = lax.axis_index("tensor")
    tensor_count = lax.axis_size("tensor")
    chosen = (owner_row == myself).astype(jnp.int32)
    my_length = jnp.sum(lens * chosen)
    capacity = 3 * tok_rows // tensor_count
    slots = jnp.arange(capacity * lax.axis_size("tensor"), dtype=jnp.int32)
    holder = slots // capacity
    within = slots % capacity
    matched = (owner_row[None, :] == holder[:, None]).astype(jnp.int32)
    first_token = jnp.sum(matched * starts[None, :], axis=1)
    span = jnp.sum(matched * lens[None, :], axis=1)
    valid = within < span
    picked = jnp.where(valid, first_token + within, 0)
    summed = lax.psum_scatter(
        jnp.take(partial_value, picked, axis=0) * valid[:, None].astype(jnp.float32),
        "tensor",
        scatter_dimension=0,
        tiled=True,
    )
    weights = (jnp.arange(capacity, dtype=jnp.int32) < my_length).astype(jnp.float32)

    def block_of(index):
        return summed[:, index * rank_width : (index + 1) * rank_width]

    pairs = ((0, 3), (1, 3), (4, 2))
    blocks = []
    for left_index, right_index in pairs:
        left_side = block_of(left_index) * weights[:, None]
        blocks.append(
            jnp.einsum(
                "ta,tb->ab", left_side, block_of(right_index), precision=lax.Precision.HIGHEST
            )
        )
    return jnp.stack(blocks, axis=0).reshape(1, 3 * rank_width * rank_width)


def solution(mesh):
    in_specs = (
        P("dp", "tensor"),
        P("dp", "tensor"),
        P("dp", "tensor"),
        P("dp", "tensor"),
        P("dp", "tensor"),
        P(("tensor", "dp"), None),
        P(("tensor", "dp"), None),
        P("dp", None),
        P("dp", None),
    )
    out_specs = P(("dp", "tensor"), None)
    ndp, ny = mesh.shape["dp"], mesh.shape["tensor"] // 2

    def program(*args):
        units, feats, rank_width = args[6].shape[0], args[5].shape[0], args[5].shape[1] // 2
        nx = math.isqrt(ndp // 2)
        fits = units % 128 == 0 and feats % 128 == 0 and rank_width == 64
        if fits and ny > 1 and nx > 1 and ndp % nx == 0 and args[0].shape[0] % 64 == 0:
            return fused(ndp // nx, nx, ny, *args)
        return per_device(*args)

    return jax.shard_map(
        program, mesh=mesh, in_specs=in_specs, out_specs=out_specs, check_vma=False
    )
```

```python
import functools
import math

import jax
import jax.numpy as jnp
from jax import lax
from jax.experimental import pallas as pl
from jax.experimental.pallas import tpu as pltpu
from jax.sharding import PartitionSpec as P

MESH = pl.DeviceIdType.MESH
NT = (((1,), (1,)), ((), ()))
TN = (((0,), (0,)), ((), ()))
F32 = jnp.float32
BF16 = jnp.bfloat16
ROWS = 32
ALONG = 2
PIECES = ((128, 64), (0, 64), (64, 64))


def kernel(
    nz, nx, ny,
    inp_h, og_h, gp_h, up_h, hg_h, pm_h, wt_h, lens, owns,
    out,
    raw, act, inp_v, og_v, pmb, wtb, acc, part, rx1, chip, sx2, rx2, full, fs,
    raw_sem, io_sem, own_sem, recv, s_up, s_dn, s_x, r_sem, t_sem, r2_sem, t2_sem,
):
    ndp = nz * nx
    me = lax.axis_index("dp")
    t = lax.axis_index("tensor")
    z, x = me // nx, me % nx
    y, c = t // 2, t % 2
    mate = y * 2 + 1 - c
    units = wt_h.shape[1]
    feats = pm_h.shape[0]
    toks = inp_h.shape[0]
    half = toks // 2
    sources = (gp_h, up_h, hg_h)

    def raw_copy(block, slot, q):
        cols = pl.ds(pl.multiple_of(block * units, 128), units)
        return pltpu.make_async_copy(sources[q].at[:, cols], raw.at[slot, q], raw_sem.at[slot, q])

    for q in range(3):
        raw_copy(0, 0, q).start()
    io = (pltpu.make_async_copy(inp_h, inp_v, io_sem.at[0]),
          pltpu.make_async_copy(og_h, og_v, io_sem.at[1]))
    pieces = 1 + len(PIECES)
    own = [pm_h] + [wt_h.at[pl.ds(row, n), :] for row, n in PIECES]

    def held(p, slot):
        return pmb.at[slot] if p == 0 else wtb.at[slot, pl.ds(*PIECES[p - 1]), :]

    barrier = pltpu.get_barrier_semaphore()

    def greet(d, s):
        pl.semaphore_signal(barrier, inc=1, device_id=(d, s), device_id_type=MESH)

    for j in range(1, nx):
        greet(z * nx + (x + j) % nx, t)
    for j in range(1, ny):
        greet(me, ((y + j) % ny) * 2 + c)
    greet(me, mate)

    @pl.when(z < nz - 1)
    def _():
        greet(me + nx, t)

    @pl.when(z > 0)
    def _():
        greet(me - nx, t)

    pl.semaphore_wait(
        barrier, nx + ny - 1 + (z < nz - 1).astype(jnp.int32) + (z > 0).astype(jnp.int32)
    )

    def remote(p, src, slot, sem, d):
        return pltpu.make_async_remote_copy(
            src_ref=src, dst_ref=held(p, slot), send_sem=sem, recv_sem=recv.at[slot, p],
            device_id=(d, t), device_id_type=MESH,
        )

    def across(p, src, slot, j):
        return remote(p, src, slot, s_x.at[slot, p, j - 1], z * nx + (x + j) % nx)

    def upward(p, src, slot):
        return remote(p, src, slot, s_up.at[slot, p], me + nx)

    def downward(p, src, slot):
        return remote(p, src, slot, s_dn.at[slot, p], me - nx)

    for p in range(pieces):
        @pl.when(z < nz - 1)
        def _():
            upward(p, own[p], me).start()

        @pl.when(z > 0)
        def _():
            downward(p, own[p], me).start()

        for j in range(1, nx):
            across(p, own[p], me, j).start()
    keep = [pltpu.make_async_copy(own[p], held(p, me), own_sem.at[p]) for p in range(pieces)]
    for p in range(pieces):
        keep[p].start()
    for copy in io:
        copy.start()
    acc[...] = jnp.zeros_like(acc)

    def elementwise(block, carry):
        slot = block % 2

        @pl.when(block + 1 < ndp)
        def _():
            for q in range(3):
                raw_copy(block + 1, 1 - slot, q).start()

        for q in range(3):
            raw_copy(block, slot, q).wait()

        def some(i, carry):
            rows = pl.ds(pl.multiple_of(i * ROWS, ROWS), ROWS)
            gate = raw[slot, 0, rows, :].astype(F32)
            up = raw[slot, 1, rows, :].astype(F32)
            grad = raw[slot, 2, rows, :].astype(F32)
            sig = 0.5 * jnp.tanh(0.5 * gate) + 0.5
            silu = gate * sig
            act[0, block, rows, :] = (grad * up * (sig + silu * (1.0 - sig))).astype(BF16)
            act[1, block, rows, :] = (grad * silu).astype(BF16)
            act[2, block, rows, :] = (silu * up).astype(BF16)
            return carry

        lax.fori_loop(0, toks // ROWS, some, 0)
        return carry

    lax.fori_loop(0, ndp, elementwise, 0)
    for copy in io:
        copy.wait()
    for p in range(pieces):
        keep[p].wait()

    def dots(slot):
        cols = pl.ds(pl.multiple_of(slot * feats, 128), feats)
        weights = pmb[slot]
        pair = wtb[slot, pl.ds(0, 128), :]
        acc[0] += lax.dot_general(act[0, slot], pair, NT, preferred_element_type=F32)
        acc[1] += lax.dot_general(act[1, slot], pair, NT, preferred_element_type=F32)
        acc[2] += jnp.dot(inp_v[:, cols], weights, preferred_element_type=F32)
        acc[3] += jnp.dot(og_v[:, cols], weights, preferred_element_type=F32)
        acc[4, :, pl.ds(0, 64)] += lax.dot_general(
            act[2, slot], wtb[slot, pl.ds(128, 64), :], NT, preferred_element_type=F32
        )

    def along(p, src_z):
        low_end = (src_z == 0) & ((z == 1) | (z == nz - 1))
        high_end = (src_z == nz - 1) & ((z == nz - 2) | (z == 0))
        return low_end | high_end if p < ALONG else src_z < 0

    def passes_up(p, src_z):
        return (src_z == 0) & ((z == 0) | (z == nz - 2)) if p < ALONG else src_z < 0

    def passes_down(p, src_z):
        return (src_z == nz - 1) & ((z == nz - 1) | (z == 1)) if p < ALONG else src_z < 0

    near = jnp.minimum(z, nz - 1 - z)

    def plane(i):
        k = (i + 1) // 2
        paired = jnp.where(i % 2 == 1, z + k, z - k)
        far = jnp.where(z < nz - 1 - z, z + i - near, z - i + near)
        return jnp.where(i <= 2 * near, paired, far)

    def step(i, carry):
        @pl.when(i < nz)
        def _():
            src_z = plane(i)
            slot = src_z * nx + x

            @pl.when(i > 0)
            def _():
                for p in range(pieces):
                    block = held(p, slot)
                    across(p, block, slot, 1).wait_recv()

                    @pl.when((src_z < z) & (z < nz - 1))
                    def _():
                        upward(p, block, slot).start()

                    @pl.when((src_z > z) & (z > 0))
                    def _():
                        downward(p, block, slot).start()

                    @pl.when(jnp.logical_not(along(p, src_z)))
                    def _():
                        for j in range(1, nx):
                            across(p, block, slot, j).start()

            dots(slot)

        @pl.when(i > 0)
        def _():
            src_z = plane(i - 1)
            for j in range(1, nx):
                slot = src_z * nx + (x + j) % nx
                for p in range(pieces):
                    block = held(p, slot)
                    across(p, block, slot, 1).wait_recv()

                    @pl.when(passes_up(p, src_z))
                    def _():
                        upward(p, block, slot).start()

                    @pl.when(passes_down(p, src_z))
                    def _():
                        downward(p, block, slot).start()

                dots(slot)

        return carry

    lax.fori_loop(0, nz + 1, step, 0)

    low = lax.broadcasted_iota(jnp.int32, (toks, 128), 1) < 64
    part[0] = jnp.where(low, acc[0], acc[1])
    part[1] = jnp.where(low, acc[2], acc[3])
    part[2] = acc[4]
    mine = pl.ds(pl.multiple_of(c * half, half), half)
    other = pl.ds(pl.multiple_of((1 - c) * half, half), half)
    first = pltpu.make_async_remote_copy(
        src_ref=part.at[:, other, :], dst_ref=rx1, send_sem=t_sem.at[0], recv_sem=r_sem.at[0],
        device_id=(me, mate), device_id_type=MESH,
    )
    first.start()
    first.wait_recv()
    both = part[:, mine, :] + rx1[...]
    chip[...] = both
    sx2[...] = both.astype(BF16)
    swaps = [
        pltpu.make_async_remote_copy(
            src_ref=sx2, dst_ref=rx2.at[j - 1], send_sem=t2_sem.at[j - 1],
            recv_sem=r2_sem.at[j - 1],
            device_id=(me, ((y + j) % ny) * 2 + c), device_id_type=MESH,
        )
        for j in range(1, ny)
    ]
    for copy in swaps:
        copy.start()
    for copy in swaps:
        copy.wait_recv()
    whole = chip[...]
    for j in range(1, ny):
        whole = whole + rx2[j - 1].astype(F32)
    full[c] = whole
    last = pltpu.make_async_remote_copy(
        src_ref=full.at[c], dst_ref=full.at[c], send_sem=t_sem.at[1], recv_sem=r_sem.at[1],
        device_id=(me, mate), device_id_type=MESH,
    )
    last.start()

    start, length, seen = jnp.int32(0), jnp.int32(0), jnp.int32(0)
    for e in range(2 * ny):
        hit = owns[0, e] == t
        start = jnp.where(hit, seen, start)
        length = jnp.where(hit, lens[0, e], length)
        seen = seen + lens[0, e]
    last.wait_recv()

    places = lax.broadcasted_iota(jnp.int32, (half, 128), 0)
    pair_one = jnp.zeros((128, 128), F32)
    pair_two = jnp.zeros((128, 128), F32)
    for h in range(2):
        token = places + h * half
        inside = (token >= start) & (token < start + length)
        model = full[h, 1]
        pair_one += lax.dot_general(
            jnp.where(inside, full[h, 0], 0.0), model, TN,
            precision=lax.Precision.HIGHEST, preferred_element_type=F32,
        )
        pair_two += lax.dot_general(
            jnp.where(inside, model, 0.0), full[h, 2], TN,
            precision=lax.Precision.HIGHEST, preferred_element_type=F32,
        )
    fs[pl.ds(0, 128), :] = pair_one
    fs[pl.ds(128, 64), :] = pair_two[64:, :]
    even = fs[pl.ds(0, 96, stride=2), :]
    odd = fs[pl.ds(1, 96, stride=2), :]
    out[...] = jnp.concatenate([even[:, :64], odd[:, :64]], axis=1)

    first.wait_send()
    last.wait_send()
    for copy in swaps:
        copy.wait_send()

    def drain(src_z, carry):
        slot = src_z * nx + x
        for p in range(pieces):
            block = held(p, slot)

            @pl.when((src_z <= z) & (z < nz - 1))
            def _():
                upward(p, block, slot).wait_send()

            @pl.when((src_z >= z) & (z > 0))
            def _():
                downward(p, block, slot).wait_send()

            @pl.when(jnp.logical_not(along(p, src_z)))
            def _():
                for j in range(1, nx):
                    across(p, block, slot, j).wait_send()

            for j in range(1, nx):
                slot_b = src_z * nx + (x + j) % nx
                block_b = held(p, slot_b)

                @pl.when(passes_up(p, src_z))
                def _():
                    upward(p, block_b, slot_b).wait_send()

                @pl.when(passes_down(p, src_z))
                def _():
                    downward(p, block_b, slot_b).wait_send()
        return carry

    lax.fori_loop(0, nz, drain, 0)


def fused(
    nz, nx, ny,
    inputs, out_grads, gate_pre, up_pre, hidden_grad, proj_model, proj_hidden, lengths, owners,
):
    ndp = nz * nx
    toks, wide = inputs.shape
    units, feats = proj_hidden.shape[0], proj_model.shape[0]
    half = toks // 2
    hbm = pl.BlockSpec(memory_space=pltpu.HBM)
    smem = pl.BlockSpec(memory_space=pltpu.SMEM)
    dma = pltpu.SemaphoreType.DMA
    out = pl.pallas_call(
        functools.partial(kernel, nz, nx, ny),
        out_shape=jax.ShapeDtypeStruct((96, 128), F32),
        in_specs=[hbm] * 7 + [smem] * 2,
        out_specs=pl.BlockSpec(memory_space=pltpu.VMEM),
        scratch_shapes=[
            pltpu.VMEM((2, 3, toks, units), BF16),
            pltpu.VMEM((3, ndp, toks, units), BF16),
            pltpu.VMEM((toks, wide), BF16),
            pltpu.VMEM((toks, wide), BF16),
            pltpu.VMEM((ndp, feats, 128), BF16),
            pltpu.VMEM((ndp, 192, units), BF16),
            pltpu.VMEM((5, toks, 128), F32),
            pltpu.VMEM((3, toks, 128), F32),
            pltpu.VMEM((3, half, 128), F32),
            pltpu.VMEM((3, half, 128), F32),
            pltpu.VMEM((3, half, 128), BF16),
            pltpu.VMEM((ny - 1, 3, half, 128), BF16),
            pltpu.VMEM((2, 3, half, 128), F32),
            pltpu.VMEM((192, 128), F32),
            dma((2, 3)),
            dma((2,)),
            dma((1 + len(PIECES),)),
            dma((ndp, 1 + len(PIECES))),
            dma((ndp, 1 + len(PIECES))),
            dma((ndp, 1 + len(PIECES))),
            dma((ndp, 1 + len(PIECES), nx - 1)),
            dma((2,)),
            dma((2,)),
            dma((ny - 1,)),
            dma((ny - 1,)),
        ],
        compiler_params=pltpu.CompilerParams(
            collective_id=0, has_side_effects=True, vmem_limit_bytes=62 << 20
        ),
    )(inputs, out_grads, gate_pre, up_pre, hidden_grad, proj_model, proj_hidden.T, lengths, owners)
    return out.reshape(1, 3 * 64 * 64)


def per_device(
    inputs, out_grads, gate_pre, up_pre, hidden_grad, proj_model, proj_hidden, lengths, owners
):
    rank_width = proj_model.shape[1] // 2
    tok_rows = inputs.shape[0]
    gate_value = gate_pre.astype(jnp.float32)
    up_value = up_pre.astype(jnp.float32)
    grad_value = hidden_grad.astype(jnp.float32)
    sigmoid_gate = jax.nn.sigmoid(gate_value)
    hidden = (gate_value * sigmoid_gate * up_value).astype(jnp.bfloat16)
    up_grad = (grad_value * gate_value * sigmoid_gate).astype(jnp.bfloat16)
    gate_grad = (
        grad_value * up_value * sigmoid_gate * (1.0 + gate_value * (1.0 - sigmoid_gate))
    ).astype(jnp.bfloat16)
    sources = (gate_grad, up_grad, hidden)
    block_rows = lax.all_gather(proj_hidden, "dp", axis=0, tiled=True)
    parts = []
    for column, source in enumerate(sources):
        parts.append(
            jnp.dot(
                source,
                block_rows[:, column * rank_width : (column + 1) * rank_width],
                preferred_element_type=jnp.float32,
            )
        )
    hidden_part = jnp.concatenate(parts, axis=1)
    block_rows = lax.all_gather(proj_model, "dp", axis=0, tiled=True)
    first_part = jnp.dot(inputs, block_rows[:, :rank_width], preferred_element_type=jnp.float32)
    second_part = jnp.dot(out_grads, block_rows[:, rank_width:], preferred_element_type=jnp.float32)
    model_part = jnp.concatenate([first_part, second_part], axis=1)
    partial_value = jnp.concatenate([hidden_part, model_part], axis=1)
    lens = lengths[0]
    owner_row = owners[0]
    starts = jnp.cumsum(lens) - lens
    myself = lax.axis_index("tensor")
    tensor_count = lax.axis_size("tensor")
    chosen = (owner_row == myself).astype(jnp.int32)
    my_length = jnp.sum(lens * chosen)
    capacity = 3 * tok_rows // tensor_count
    slots = jnp.arange(capacity * lax.axis_size("tensor"), dtype=jnp.int32)
    holder = slots // capacity
    within = slots % capacity
    matched = (owner_row[None, :] == holder[:, None]).astype(jnp.int32)
    first_token = jnp.sum(matched * starts[None, :], axis=1)
    span = jnp.sum(matched * lens[None, :], axis=1)
    valid = within < span
    picked = jnp.where(valid, first_token + within, 0)
    summed = lax.psum_scatter(
        jnp.take(partial_value, picked, axis=0) * valid[:, None].astype(jnp.float32),
        "tensor",
        scatter_dimension=0,
        tiled=True,
    )
    weights = (jnp.arange(capacity, dtype=jnp.int32) < my_length).astype(jnp.float32)

    def block_of(index):
        return summed[:, index * rank_width : (index + 1) * rank_width]

    pairs = ((0, 3), (1, 3), (4, 2))
    blocks = []
    for left_index, right_index in pairs:
        left_side = block_of(left_index) * weights[:, None]
        blocks.append(
            jnp.einsum(
                "ta,tb->ab", left_side, block_of(right_index), precision=lax.Precision.HIGHEST
            )
        )
    return jnp.stack(blocks, axis=0).reshape(1, 3 * rank_width * rank_width)


def solution(mesh):
    in_specs = (
        P("dp", "tensor"),
        P("dp", "tensor"),
        P("dp", "tensor"),
        P("dp", "tensor"),
        P("dp", "tensor"),
        P(("tensor", "dp"), None),
        P(("tensor", "dp"), None),
        P("dp", None),
        P("dp", None),
    )
    out_specs = P(("dp", "tensor"), None)
    ndp, ny = mesh.shape["dp"], mesh.shape["tensor"] // 2

    def program(*args):
        units, feats, rank_width = args[6].shape[0], args[5].shape[0], args[5].shape[1] // 2
        nx = math.isqrt(ndp // 2)
        fits = units % 128 == 0 and feats % 128 == 0 and rank_width == 64
        if fits and ny > 1 and nx > 1 and ndp // nx > 3 and ndp % nx == 0 and args[0].shape[0] % 64 == 0:
            return fused(ndp // nx, nx, ny, *args)
        return per_device(*args)

    return jax.shard_map(
        program, mesh=mesh, in_specs=in_specs, out_specs=out_specs, check_vma=False
    )
```

```python
import functools
import math

import jax
import jax.numpy as jnp
from jax import lax
from jax.experimental import pallas as pl
from jax.experimental.pallas import tpu as pltpu
from jax.sharding import PartitionSpec as P

MESH = pl.DeviceIdType.MESH
NT = (((1,), (1,)), ((), ()))
TN = (((0,), (0,)), ((), ()))
F32 = jnp.float32
BF16 = jnp.bfloat16
ROWS = 32
ALONG = 2
PIECES = ((128, 64), (0, 64), (64, 64))


def kernel(
    nz, nx, ny,
    inp_h, og_h, gp_h, up_h, hg_h, pm_h, wt_h, lens, owns,
    out,
    raw, act, inp_v, og_v, pmb, wtb, acc, part, rx1, chip, sx2, rx2, full, fs,
    raw_sem, io_sem, own_sem, recv, s_up, s_dn, s_x, r_sem, t_sem, r2_sem, t2_sem,
):
    ndp = nz * nx
    me = lax.axis_index("dp")
    t = lax.axis_index("tensor")
    z, x = me // nx, me % nx
    y, c = t // 2, t % 2
    mate = y * 2 + 1 - c
    units = wt_h.shape[1]
    feats = pm_h.shape[0]
    toks = inp_h.shape[0]
    half = toks // 2
    sources = (gp_h, up_h, hg_h)

    def raw_copy(block, slot, q):
        cols = pl.ds(pl.multiple_of(block * units, 128), units)
        return pltpu.make_async_copy(sources[q].at[:, cols], raw.at[slot, q], raw_sem.at[slot, q])

    for q in range(3):
        raw_copy(0, 0, q).start()
    io = (pltpu.make_async_copy(inp_h, inp_v, io_sem.at[0]),
          pltpu.make_async_copy(og_h, og_v, io_sem.at[1]))
    pieces = 1 + len(PIECES)
    own = [pm_h] + [wt_h.at[pl.ds(row, n), :] for row, n in PIECES]

    def held(p, slot):
        return pmb.at[slot] if p == 0 else wtb.at[slot, pl.ds(*PIECES[p - 1]), :]

    barrier = pltpu.get_barrier_semaphore()

    def greet(d, s):
        pl.semaphore_signal(barrier, inc=1, device_id=(d, s), device_id_type=MESH)

    for j in range(1, nx):
        greet(z * nx + (x + j) % nx, t)
    for j in range(1, ny):
        greet(me, ((y + j) % ny) * 2 + c)
    greet(me, mate)

    @pl.when(z < nz - 1)
    def _():
        greet(me + nx, t)

    @pl.when(z > 0)
    def _():
        greet(me - nx, t)

    pl.semaphore_wait(
        barrier, nx + ny - 1 + (z < nz - 1).astype(jnp.int32) + (z > 0).astype(jnp.int32)
    )

    def remote(p, src, slot, sem, d):
        return pltpu.make_async_remote_copy(
            src_ref=src, dst_ref=held(p, slot), send_sem=sem, recv_sem=recv.at[slot, p],
            device_id=(d, t), device_id_type=MESH,
        )

    def across(p, src, slot, j):
        return remote(p, src, slot, s_x.at[slot, p, j - 1], z * nx + (x + j) % nx)

    def upward(p, src, slot):
        return remote(p, src, slot, s_up.at[slot, p], me + nx)

    def downward(p, src, slot):
        return remote(p, src, slot, s_dn.at[slot, p], me - nx)

    for p in range(pieces):
        @pl.when(z < nz - 1)
        def _():
            upward(p, own[p], me).start()

        @pl.when(z > 0)
        def _():
            downward(p, own[p], me).start()

        for j in range(1, nx):
            across(p, own[p], me, j).start()
    keep = [pltpu.make_async_copy(own[p], held(p, me), own_sem.at[p]) for p in range(pieces)]
    for p in range(pieces):
        keep[p].start()
    for copy in io:
        copy.start()
    acc[...] = jnp.zeros_like(acc)

    def elementwise(block, carry):
        slot = block % 2

        @pl.when(block + 1 < ndp)
        def _():
            for q in range(3):
                raw_copy(block + 1, 1 - slot, q).start()

        for q in range(3):
            raw_copy(block, slot, q).wait()

        def some(i, carry):
            rows = pl.ds(pl.multiple_of(i * ROWS, ROWS), ROWS)
            gate = raw[slot, 0, rows, :].astype(F32)
            up = raw[slot, 1, rows, :].astype(F32)
            grad = raw[slot, 2, rows, :].astype(F32)
            sig = 0.5 * jnp.tanh(0.5 * gate) + 0.5
            silu = gate * sig
            act[0, block, rows, :] = (grad * up * (sig + silu * (1.0 - sig))).astype(BF16)
            act[1, block, rows, :] = (grad * silu).astype(BF16)
            act[2, block, rows, :] = (silu * up).astype(BF16)
            return carry

        lax.fori_loop(0, toks // ROWS, some, 0)
        return carry

    lax.fori_loop(0, ndp, elementwise, 0)
    for copy in io:
        copy.wait()
    for p in range(pieces):
        keep[p].wait()

    def dots(slot):
        cols = pl.ds(pl.multiple_of(slot * feats, 128), feats)
        weights = pmb[slot]
        pair = wtb[slot, pl.ds(0, 128), :]
        acc[0] += lax.dot_general(act[0, slot], pair, NT, preferred_element_type=F32)
        acc[1] += lax.dot_general(act[1, slot], pair, NT, preferred_element_type=F32)
        acc[2] += jnp.dot(inp_v[:, cols], weights, preferred_element_type=F32)
        acc[3] += jnp.dot(og_v[:, cols], weights, preferred_element_type=F32)
        acc[4, :, pl.ds(0, 64)] += lax.dot_general(
            act[2, slot], wtb[slot, pl.ds(128, 64), :], NT, preferred_element_type=F32
        )

    def along(p, src_z):
        low_end = (src_z == 0) & ((z == 1) | (z == nz - 1))
        high_end = (src_z == nz - 1) & ((z == nz - 2) | (z == 0))
        return low_end | high_end if p < ALONG else src_z < 0

    def passes_up(p, src_z):
        return (src_z == 0) & ((z == 0) | (z == nz - 2)) if p < ALONG else src_z < 0

    def passes_down(p, src_z):
        return (src_z == nz - 1) & ((z == nz - 1) | (z == 1)) if p < ALONG else src_z < 0

    near = jnp.minimum(z, nz - 1 - z)

    def plane(i):
        k = (i + 1) // 2
        paired = jnp.where(i % 2 == 1, z + k, z - k)
        far = jnp.where(z < nz - 1 - z, z + i - near, z - i + near)
        return jnp.where(i <= 2 * near, paired, far)

    def step(i, carry):
        @pl.when(i < nz)
        def _():
            src_z = plane(i)
            slot = src_z * nx + x

            @pl.when(i > 0)
            def _():
                for p in range(pieces):
                    block = held(p, slot)
                    across(p, block, slot, 1).wait_recv()

                    @pl.when((src_z < z) & (z < nz - 1))
                    def _():
                        upward(p, block, slot).start()

                    @pl.when((src_z > z) & (z > 0))
                    def _():
                        downward(p, block, slot).start()

                    @pl.when(jnp.logical_not(along(p, src_z)))
                    def _():
                        for j in range(1, nx):
                            across(p, block, slot, j).start()

            dots(slot)

        @pl.when(i > 0)
        def _():
            src_z = plane(i - 1)
            for j in range(1, nx):
                slot = src_z * nx + (x + j) % nx
                for p in range(pieces):
                    block = held(p, slot)
                    across(p, block, slot, 1).wait_recv()

                    @pl.when(passes_up(p, src_z))
                    def _():
                        upward(p, block, slot).start()

                    @pl.when(passes_down(p, src_z))
                    def _():
                        downward(p, block, slot).start()

                dots(slot)

        return carry

    lax.fori_loop(0, nz + 1, step, 0)

    low = lax.broadcasted_iota(jnp.int32, (toks, 128), 1) < 64
    part[0] = jnp.where(low, acc[0], acc[1])
    part[1] = jnp.where(low, acc[2], acc[3])
    part[2] = acc[4]
    mine = pl.ds(pl.multiple_of(c * half, half), half)
    other = pl.ds(pl.multiple_of((1 - c) * half, half), half)
    first = [
        pltpu.make_async_remote_copy(
            src_ref=part.at[k, other, :], dst_ref=rx1.at[k], send_sem=t_sem.at[0, k],
            recv_sem=r_sem.at[0, k], device_id=(me, mate), device_id_type=MESH,
        )
        for k in range(3)
    ]
    swaps = [
        [
            pltpu.make_async_remote_copy(
                src_ref=sx2.at[k], dst_ref=rx2.at[j - 1, k], send_sem=t2_sem.at[j - 1, k],
                recv_sem=r2_sem.at[j - 1, k],
                device_id=(me, ((y + j) % ny) * 2 + c), device_id_type=MESH,
            )
            for j in range(1, ny)
        ]
        for k in range(3)
    ]
    last = [
        pltpu.make_async_remote_copy(
            src_ref=full.at[c, k], dst_ref=full.at[c, k], send_sem=t_sem.at[1, k],
            recv_sem=r_sem.at[1, k], device_id=(me, mate), device_id_type=MESH,
        )
        for k in range(3)
    ]
    for copy in first:
        copy.start()
    for k in range(3):
        first[k].wait_recv()
        both = part[k, mine, :] + rx1[k]
        chip[k] = both
        sx2[k] = both.astype(BF16)
        for copy in swaps[k]:
            copy.start()
    for k in range(3):
        whole = chip[k]
        for j in range(1, ny):
            swaps[k][j - 1].wait_recv()
            whole = whole + rx2[j - 1, k].astype(F32)
        full[c, k] = whole
        last[k].start()

    start, length, seen = jnp.int32(0), jnp.int32(0), jnp.int32(0)
    for e in range(2 * ny):
        hit = owns[0, e] == t
        start = jnp.where(hit, seen, start)
        length = jnp.where(hit, lens[0, e], length)
        seen = seen + lens[0, e]
    for copy in last:
        copy.wait_recv()

    places = lax.broadcasted_iota(jnp.int32, (half, 128), 0)
    pair_one = jnp.zeros((128, 128), F32)
    pair_two = jnp.zeros((128, 128), F32)
    for h in range(2):
        token = places + h * half
        inside = (token >= start) & (token < start + length)
        model = full[h, 1]
        pair_one += lax.dot_general(
            jnp.where(inside, full[h, 0], 0.0), model, TN,
            precision=lax.Precision.HIGHEST, preferred_element_type=F32,
        )
        pair_two += lax.dot_general(
            jnp.where(inside, model, 0.0), full[h, 2], TN,
            precision=lax.Precision.HIGHEST, preferred_element_type=F32,
        )
    fs[pl.ds(0, 128), :] = pair_one
    fs[pl.ds(128, 64), :] = pair_two[64:, :]
    even = fs[pl.ds(0, 96, stride=2), :]
    odd = fs[pl.ds(1, 96, stride=2), :]
    out[...] = jnp.concatenate([even[:, :64], odd[:, :64]], axis=1)

    for k in range(3):
        first[k].wait_send()
        last[k].wait_send()
        for copy in swaps[k]:
            copy.wait_send()

    def drain(src_z, carry):
        slot = src_z * nx + x
        for p in range(pieces):
            block = held(p, slot)

            @pl.when((src_z <= z) & (z < nz - 1))
            def _():
                upward(p, block, slot).wait_send()

            @pl.when((src_z >= z) & (z > 0))
            def _():
                downward(p, block, slot).wait_send()

            @pl.when(jnp.logical_not(along(p, src_z)))
            def _():
                for j in range(1, nx):
                    across(p, block, slot, j).wait_send()

            for j in range(1, nx):
                slot_b = src_z * nx + (x + j) % nx
                block_b = held(p, slot_b)

                @pl.when(passes_up(p, src_z))
                def _():
                    upward(p, block_b, slot_b).wait_send()

                @pl.when(passes_down(p, src_z))
                def _():
                    downward(p, block_b, slot_b).wait_send()
        return carry

    lax.fori_loop(0, nz, drain, 0)


def fused(
    nz, nx, ny,
    inputs, out_grads, gate_pre, up_pre, hidden_grad, proj_model, proj_hidden, lengths, owners,
):
    ndp = nz * nx
    toks, wide = inputs.shape
    units, feats = proj_hidden.shape[0], proj_model.shape[0]
    half = toks // 2
    hbm = pl.BlockSpec(memory_space=pltpu.HBM)
    smem = pl.BlockSpec(memory_space=pltpu.SMEM)
    dma = pltpu.SemaphoreType.DMA
    out = pl.pallas_call(
        functools.partial(kernel, nz, nx, ny),
        out_shape=jax.ShapeDtypeStruct((96, 128), F32),
        in_specs=[hbm] * 7 + [smem] * 2,
        out_specs=pl.BlockSpec(memory_space=pltpu.VMEM),
        scratch_shapes=[
            pltpu.VMEM((2, 3, toks, units), BF16),
            pltpu.VMEM((3, ndp, toks, units), BF16),
            pltpu.VMEM((toks, wide), BF16),
            pltpu.VMEM((toks, wide), BF16),
            pltpu.VMEM((ndp, feats, 128), BF16),
            pltpu.VMEM((ndp, 192, units), BF16),
            pltpu.VMEM((5, toks, 128), F32),
            pltpu.VMEM((3, toks, 128), F32),
            pltpu.VMEM((3, half, 128), F32),
            pltpu.VMEM((3, half, 128), F32),
            pltpu.VMEM((3, half, 128), BF16),
            pltpu.VMEM((ny - 1, 3, half, 128), BF16),
            pltpu.VMEM((2, 3, half, 128), F32),
            pltpu.VMEM((192, 128), F32),
            dma((2, 3)),
            dma((2,)),
            dma((1 + len(PIECES),)),
            dma((ndp, 1 + len(PIECES))),
            dma((ndp, 1 + len(PIECES))),
            dma((ndp, 1 + len(PIECES))),
            dma((ndp, 1 + len(PIECES), nx - 1)),
            dma((2, 3)),
            dma((2, 3)),
            dma((ny - 1, 3)),
            dma((ny - 1, 3)),
        ],
        compiler_params=pltpu.CompilerParams(
            collective_id=0, has_side_effects=True, vmem_limit_bytes=62 << 20
        ),
    )(inputs, out_grads, gate_pre, up_pre, hidden_grad, proj_model, proj_hidden.T, lengths, owners)
    return out.reshape(1, 3 * 64 * 64)


def per_device(
    inputs, out_grads, gate_pre, up_pre, hidden_grad, proj_model, proj_hidden, lengths, owners
):
    rank_width = proj_model.shape[1] // 2
    tok_rows = inputs.shape[0]
    gate_value = gate_pre.astype(jnp.float32)
    up_value = up_pre.astype(jnp.float32)
    grad_value = hidden_grad.astype(jnp.float32)
    sigmoid_gate = jax.nn.sigmoid(gate_value)
    hidden = (gate_value * sigmoid_gate * up_value).astype(jnp.bfloat16)
    up_grad = (grad_value * gate_value * sigmoid_gate).astype(jnp.bfloat16)
    gate_grad = (
        grad_value * up_value * sigmoid_gate * (1.0 + gate_value * (1.0 - sigmoid_gate))
    ).astype(jnp.bfloat16)
    sources = (gate_grad, up_grad, hidden)
    block_rows = lax.all_gather(proj_hidden, "dp", axis=0, tiled=True)
    parts = []
    for column, source in enumerate(sources):
        parts.append(
            jnp.dot(
                source,
                block_rows[:, column * rank_width : (column + 1) * rank_width],
                preferred_element_type=jnp.float32,
            )
        )
    hidden_part = jnp.concatenate(parts, axis=1)
    block_rows = lax.all_gather(proj_model, "dp", axis=0, tiled=True)
    first_part = jnp.dot(inputs, block_rows[:, :rank_width], preferred_element_type=jnp.float32)
    second_part = jnp.dot(out_grads, block_rows[:, rank_width:], preferred_element_type=jnp.float32)
    model_part = jnp.concatenate([first_part, second_part], axis=1)
    partial_value = jnp.concatenate([hidden_part, model_part], axis=1)
    lens = lengths[0]
    owner_row = owners[0]
    starts = jnp.cumsum(lens) - lens
    myself = lax.axis_index("tensor")
    tensor_count = lax.axis_size("tensor")
    chosen = (owner_row == myself).astype(jnp.int32)
    my_length = jnp.sum(lens * chosen)
    capacity = 3 * tok_rows // tensor_count
    slots = jnp.arange(capacity * lax.axis_size("tensor"), dtype=jnp.int32)
    holder = slots // capacity
    within = slots % capacity
    matched = (owner_row[None, :] == holder[:, None]).astype(jnp.int32)
    first_token = jnp.sum(matched * starts[None, :], axis=1)
    span = jnp.sum(matched * lens[None, :], axis=1)
    valid = within < span
    picked = jnp.where(valid, first_token + within, 0)
    summed = lax.psum_scatter(
        jnp.take(partial_value, picked, axis=0) * valid[:, None].astype(jnp.float32),
        "tensor",
        scatter_dimension=0,
        tiled=True,
    )
    weights = (jnp.arange(capacity, dtype=jnp.int32) < my_length).astype(jnp.float32)

    def block_of(index):
        return summed[:, index * rank_width : (index + 1) * rank_width]

    pairs = ((0, 3), (1, 3), (4, 2))
    blocks = []
    for left_index, right_index in pairs:
        left_side = block_of(left_index) * weights[:, None]
        blocks.append(
            jnp.einsum(
                "ta,tb->ab", left_side, block_of(right_index), precision=lax.Precision.HIGHEST
            )
        )
    return jnp.stack(blocks, axis=0).reshape(1, 3 * rank_width * rank_width)


def solution(mesh):
    in_specs = (
        P("dp", "tensor"),
        P("dp", "tensor"),
        P("dp", "tensor"),
        P("dp", "tensor"),
        P("dp", "tensor"),
        P(("tensor", "dp"), None),
        P(("tensor", "dp"), None),
        P("dp", None),
        P("dp", None),
    )
    out_specs = P(("dp", "tensor"), None)
    ndp, ny = mesh.shape["dp"], mesh.shape["tensor"] // 2

    def program(*args):
        units, feats, rank_width = args[6].shape[0], args[5].shape[0], args[5].shape[1] // 2
        nx = math.isqrt(ndp // 2)
        fits = units % 128 == 0 and feats % 128 == 0 and rank_width == 64
        if fits and ny > 1 and nx > 1 and ndp // nx > 3 and ndp % nx == 0 and args[0].shape[0] % 64 == 0:
            return fused(ndp // nx, nx, ny, *args)
        return per_device(*args)

    return jax.shard_map(
        program, mesh=mesh, in_specs=in_specs, out_specs=out_specs, check_vma=False
    )
```
